32 devices in a mesh: group: 4 (over y, x), fsdp: 8 (over z, core).
Axes of the slice: x: 2, y: 2, z: 4, core: 2. Of those that a mesh axis runs over, the one named last changes fastest.
Arguments:
- inputs: bfloat16 [8192, 4096], P('group', 'fsdp'), may hold values from -6 to 6
- norm_gain: bfloat16 [4096], P('fsdp'), may hold values from 0.099609375 to 1.8984375
- cotangent: bfloat16 [8192, 16384], P('group', 'fsdp'), may hold values from -0.03125 to 0.03125
- owners: int32 [32, 4], P('fsdp'), may hold values from 0 to 3, each once within a row
- refresh: int32 [8, 32], P('group', 'fsdp'), may hold values 0 or 1
- left_stats: float32 [4096, 16384], P('group', 'fsdp'), may hold values from -1 to 16, as said below
- right_stats: float32 [4096, 16384], P('group', 'fsdp'), may hold values from -1 to 16, as said below
- left_inverse: float32 [4096, 16384], P('group', 'fsdp'), may hold values from -1 to 8, as said below
- right_inverse: float32 [4096, 16384], P('group', 'fsdp'), may hold values from -1 to 8, as said below
Outputs:
- update: bfloat16 [4096, 16384], P('group', 'fsdp')
- left_accum: float32 [4096, 16384], P('group', 'fsdp')
- right_accum: float32 [4096, 16384], P('group', 'fsdp')
- left_refreshed: float32 [4096, 16384], P('group', 'fsdp')
- right_refreshed: float32 [4096, 16384], P('group', 'fsdp')
The draws below stay inside these ranges and needn't reach their ends.
Inputs may be any that keep to these rules, and one draw needn't show every extreme that they name: Each row owners[c] is a permutation of 0 to 4 - 1. `left_stats`: symmetric within each 512 x 512 block, diagonal entries at least 1. `right_stats`: symmetric within each 512 x 512 block, diagonal entries at least 1. `left_inverse`: symmetric within each 512 x 512 block. `right_inverse`: symmetric within each 512 x 512 block.
All inputs are finite; a program needn't handle non-finite values. No bound on the sum of `refresh` on one device may be relied on, other than what follows from the above.
Results may differ from the reference program's by a relative error of at most 0.013.
Values may be sent and summed in bfloat16 or wider, within the bound.
A program may use at most 256 MiB of HBM per device.

```python
import jax
import jax.numpy as jnp
from jax import lax

D = 4096
F = 16384
BLK = 512
TOK_ROW = 2048
ITERS = 2
TOKENS = 8192
ROW_BLOCKS = 8
COL_BLOCKS = 32
N_GROUP = 4


def symmetric_blocks(key, lowest, highest):
    block_order = BLK
    row_count = D // block_order
    col_count = F // block_order
    half_width = 0.98 * lowest / block_order
    off_diagonal = jax.random.uniform(jax.random.fold_in(key, 1), (row_count, block_order, col_count, block_order), jnp.float32, -half_width, half_width)
    off_diagonal = 0.5 * (off_diagonal + off_diagonal.transpose(0, 3, 2, 1))
    log_values = jax.random.uniform(jax.random.fold_in(key, 2), (row_count, block_order, col_count, 1), jnp.float32, jnp.log(lowest), jnp.log(highest))
    on_diagonal = lax.broadcasted_iota(jnp.int32, (1, block_order, 1, block_order), 1) == lax.broadcasted_iota(jnp.int32, (1, block_order, 1, block_order), 3)
    filled = jnp.where(on_diagonal, jnp.exp(log_values), off_diagonal)
    return filled.reshape(row_count * block_order, col_count * block_order)


def draw_left_stats(key, part):
    return symmetric_blocks(jax.random.fold_in(key, 11), 1.0, 4.0)


def draw_right_stats(key, part):
    return symmetric_blocks(jax.random.fold_in(key, 12), 1.0, 4.0)


def draw_left_inverse(key, part):
    return symmetric_blocks(jax.random.fold_in(key, 13), 0.5, 2.0)


def draw_right_inverse(key, part):
    return symmetric_blocks(jax.random.fold_in(key, 14), 0.5, 2.0)


def touch_ends(entries, own_key, low, largest):
    longest = entries.shape.index(max(entries.shape))
    spots = []
    for shift in (0, 1):
        where = [jax.random.randint(jax.random.fold_in(own_key, axis), (), 0, length) for axis, length in enumerate(entries.shape)]
        where[longest] = (where[longest] + shift) % entries.shape[longest]
        spots.append(tuple(where))
    return entries.at[spots[0]].set(low).at[spots[1]].set(largest)


def shard_levels(stream_key, extent, pieces, least, largest):
    loudness = 1.0
    for position, shards_of in pieces:
        draws = jax.random.uniform(jax.random.fold_in(jax.random.fold_in(stream_key, 6), position), (shards_of,), jnp.float32, least / len(pieces), largest / len(pieces))
        loudness = loudness * jnp.repeat(jnp.exp(draws), extent[position] // shards_of).reshape((-1,) + (1,) * (len(extent) - 1 - position))
    return loudness


def gaussian(key, extent, scale, reach, pieces=(), kind=jnp.bfloat16):
    gain = shard_levels(key, extent, pieces, -0.22, 0.18) if pieces else 1.0
    entries = jax.random.normal(key, extent, jnp.float32) * scale * gain
    return jnp.minimum(jnp.maximum(entries, -reach), reach).astype(kind)


def setup_inputs(seed: int = 0) -> dict:
    key_of = jax.random.split(jax.random.key(seed), 10)
    return {
        "inputs": gaussian(key_of[0], (TOKENS, D), 1.0, 6.0, ((0, 4), (1, 8))),
        "norm_gain": jnp.clip(1.0 + 0.18 * jax.random.normal(key_of[1], (D,), jnp.float32), 0.099609375, 1.8984375).astype(jnp.bfloat16),
        "cotangent": gaussian(key_of[2], (TOKENS, F), ((25 * TOKENS) ** -0.5), 0.03125, ((0, 4), (1, 8))),
        "owners": jax.vmap(lambda own: jax.random.permutation(own, N_GROUP))(jax.random.split(key_of[3], COL_BLOCKS)).reshape((COL_BLOCKS, N_GROUP)).astype(jnp.int32),
        "refresh": touch_ends((jax.random.randint(key_of[4], (ROW_BLOCKS, COL_BLOCKS), 0, 4) < 1).astype(jnp.int32), jax.random.fold_in(key_of[4], 1), 0, 1),
        "left_stats": draw_left_stats(jax.random.fold_in(key_of[9], 71), 0),
        "right_stats": draw_right_stats(jax.random.fold_in(key_of[9], 71), 0),
        "left_inverse": draw_left_inverse(jax.random.fold_in(key_of[9], 71), 0),
        "right_inverse": draw_right_inverse(jax.random.fold_in(key_of[9], 71), 0),
    }


NORM_EPSILON = 1e-05
SCALE_EPSILON = 1e-06
DECAY_RATE = 0.95
RIDGE_TERM = 1e-06
HIGHEST = lax.Precision.HIGHEST

def to_blocks(matrix, block_order):
    row_count, col_count = matrix.shape
    shaped = matrix.reshape(row_count // block_order, block_order, col_count // block_order, block_order)
    return shaped.transpose(0, 2, 1, 3).reshape(-1, block_order, block_order)

def from_blocks(blocks, row_count, col_count):
    block_order = blocks.shape[-1]
    shaped = blocks.reshape(row_count // block_order, col_count // block_order, block_order, block_order)
    return shaped.transpose(0, 2, 1, 3).reshape(row_count, col_count)

def inverse_fourth_root(statistic):
    block_order = statistic.shape[0]
    identity = jnp.eye(block_order, dtype=statistic.dtype)
    matrix = statistic + RIDGE_TERM * identity
    scaling = 2.5 / jnp.sqrt(jnp.sum(matrix * matrix))
    inverse_root = scaling ** 0.25 * identity
    scaled = scaling * matrix
    for iteration in range(ITERS):
        factor = 1.25 * identity - 0.25 * scaled
        inverse_root = jnp.dot(inverse_root, factor, precision=HIGHEST)
        if iteration + 1 < ITERS:
            square = jnp.dot(factor, factor, precision=HIGHEST)
            scaled = jnp.dot(jnp.dot(square, square, precision=HIGHEST), scaled, precision=HIGHEST)
    return inverse_root

def block_step(operands):
    grad_block, left_old, right_old, left_root, right_root, refresh_flag = operands
    left_gram = lax.dot_general(grad_block, grad_block, (((1,), (1,)), ((), ())), preferred_element_type=jnp.float32)
    right_gram = lax.dot_general(grad_block, grad_block, (((0,), (0,)), ((), ())), preferred_element_type=jnp.float32)
    left_accum = DECAY_RATE * left_old + (1.0 - DECAY_RATE) * left_gram
    right_accum = DECAY_RATE * right_old + (1.0 - DECAY_RATE) * right_gram
    local_grad = grad_block.astype(jnp.float32)
    conditioned = jnp.dot(jnp.dot(left_root, local_grad, precision=HIGHEST), right_root, precision=HIGHEST)
    own_update = (conditioned * lax.rsqrt(jnp.mean(conditioned * conditioned) + SCALE_EPSILON)).astype(jnp.bfloat16)

    def recompute(unused):
        return (inverse_fourth_root(left_accum), inverse_fourth_root(right_accum))

    def keep_old(unused):
        return (left_root, right_root)
    left_new, right_new = lax.cond(refresh_flag > 0, recompute, keep_old, 0)
    return (own_update, left_accum, right_accum, left_new, right_new)

def reference(inputs, norm_gain, cotangent, owners, refresh, left_stats, right_stats, left_inverse, right_inverse):
    values = inputs.astype(jnp.float32)
    scales = lax.rsqrt(lax.optimization_barrier(jnp.mean(values * values, axis=1)) + NORM_EPSILON)
    normed = (values * scales[:, None] * norm_gain.astype(jnp.float32)[None, :]).astype(jnp.bfloat16)
    summed = jnp.zeros((D, F), jnp.float32)
    for group_row in range(N_GROUP):
        rows_in = normed[group_row * TOK_ROW:(group_row + 1) * TOK_ROW]
        grads_in = cotangent[group_row * TOK_ROW:(group_row + 1) * TOK_ROW]
        partial_value = lax.dot_general(rows_in, grads_in, (((0,), (0,)), ((), ())), preferred_element_type=jnp.float32)
        summed = summed + partial_value.astype(jnp.bfloat16).astype(jnp.float32)
    gradient = summed.astype(jnp.bfloat16)
    slab_rows = D // N_GROUP
    col_blocks = F // BLK
    rank_list = jnp.arange(N_GROUP, dtype=jnp.int32)
    inverse_map = lax.optimization_barrier(jnp.sum(jnp.where(owners[:, :, None] == rank_list[None, None, :], rank_list[None, :, None], 0), axis=1)).astype(jnp.int32)
    slab_shape = (N_GROUP, slab_rows, col_blocks, BLK)
    gather_index = jnp.broadcast_to(inverse_map.T[:, None, :, None], slab_shape)
    own_grad = jnp.take_along_axis(gradient.reshape(slab_shape), gather_index, axis=0).reshape(D, F)
    results = lax.map(block_step, (to_blocks(own_grad, BLK), to_blocks(left_stats, BLK), to_blocks(right_stats, BLK), to_blocks(left_inverse, BLK), to_blocks(right_inverse, BLK), refresh.reshape(-1)))
    own_update, left_accum, right_accum, left_new, right_new = results
    own_update = from_blocks(own_update, D, F)
    back_index = jnp.broadcast_to(owners.astype(jnp.int32).T[:, None, :, None], slab_shape)
    update = jnp.take_along_axis(own_update.reshape(slab_shape), back_index, axis=0).reshape(D, F)
    return (update, from_blocks(left_accum, D, F), from_blocks(right_accum, D, F), from_blocks(left_new, D, F), from_blocks(right_new, D, F))
```

```python
import functools
import jax
import jax.numpy as jnp
from jax import lax
from jax.experimental import pallas as pl
from jax.experimental.pallas import tpu as pltpu
from jax.sharding import PartitionSpec as P

BLK = 512
NORM_EPSILON = 1e-05
MESH = pl.DeviceIdType.MESH
RING = 4


def remote(src, dst, send_sem, recv_sem, device):
    return pltpu.make_async_remote_copy(
        src_ref=src, dst_ref=dst, send_sem=send_sem, recv_sem=recv_sem,
        device_id=device, device_id_type=MESH,
    )


def grad_kernel(G, F, NC, LEAD, TN, owners, gain, x_hbm, cot_hbm, og, xbuf, xt, gcol, cotv, ga, ssall, res, *rest):
    nb = G.bit_length() - 1
    sends, recvs, curs = rest[:nb], rest[nb:2 * nb], rest[2 * nb:3 * nb - 1]
    lsem, ss_send, ss_recv, gs, gl, gr, rs_send, rs_recv = rest[3 * nb - 1:]
    T, S = xbuf.shape
    N = cotv.shape[1]
    D = S * F
    L, q, rk, Nh = F // 2, F // G, S // NC, N // 2
    R, M = q * rk, F * rk
    W = min(BLK, Nh)
    g, f = lax.axis_index("group"), lax.axis_index("fsdp")
    l, core = f // 2, f % 2
    sib = f + 1 - 2 * core

    def bit(b):
        return (g // (1 << b)) % 2

    def partner(b):
        return g + (1 - 2 * bit(b)) * (1 << b)

    x_copy = pltpu.make_async_copy(x_hbm, xbuf, lsem.at[0])
    x_copy.start()
    cot_copy = pltpu.make_async_copy(cot_hbm, cotv, lsem.at[1])
    cot_copy.start()

    barrier = pltpu.get_barrier_semaphore()
    for d in range(1, F):
        pl.semaphore_signal(barrier, inc=1, device_id=(g, (f + d) % F), device_id_type=MESH)
    for b in range(nb):
        pl.semaphore_signal(barrier, inc=1, device_id=(partner(b), f), device_id_type=MESH)

    gcol[...] = jnp.broadcast_to(gain[...].astype(jnp.float32), (128, S)).T
    x_copy.wait()
    TT = 256
    for i in range(T // TT):
        v = xbuf[i * TT:(i + 1) * TT, :].astype(jnp.float32).T
        ssall[f, :, i * TT:(i + 1) * TT] = jnp.sum(v * v, axis=0, keepdims=True)
        xt[:, i * TT:(i + 1) * TT] = v.astype(jnp.bfloat16)
    pl.semaphore_wait(barrier, F - 1 + nb)

    def ss_copy(slot, peer, d):
        return remote(ssall.at[slot], ssall.at[slot], ss_send.at[d - 1], ss_recv.at[slot], (g, peer))

    for d in range(1, F):
        ss_copy(f, (f + d) % F, d).start()
    for d in range(1, F):
        peer = (f + d) % F
        ss_copy(peer, peer, d).wait_recv()
    total = jnp.sum(ssall[...], axis=0)
    scale = lax.rsqrt(total * (1.0 / D) + NORM_EPSILON)

    def piece(k, shard, send_sem, peer):
        return remote(ga.at[k, shard], ga.at[k, shard], send_sem, gr.at[k, shard], (g, peer))

    def onward(k, src, go, peer, then):
        shard, ring = 2 * src + core, k % RING

        @pl.when(go)
        def _():
            then(piece(k, shard, gs.at[ring, src, 0], peer))

        then(piece(k, shard, gs.at[ring, src, 1], sib))

    def own(k, then):
        onward(k, l, l < L - 1, f + 2, then)

        @pl.when(l > 0)
        def _():
            then(piece(k, f, gl.at[k % RING], f - 2))

    def forward(k, d, then, receive):
        @pl.when(l - d >= 0)
        def _():
            if receive:
                piece(k, 2 * (l - d) + core, gs.at[0, 0, 0], sib).wait_recv()
            onward(k, l - d, l < L - 1, f + 2, then)

        @pl.when(l + d <= L - 1)
        def _():
            if receive:
                piece(k, 2 * (l + d) + core, gs.at[0, 0, 0], sib).wait_recv()
            onward(k, l + d, l > 0, f - 2, then)

    def start(copy):
        copy.start()

    def finish(copy):
        copy.wait_send()

    def wait_sibling(k):
        for src in range(L):
            piece(k, 2 * src + 1 - core, gs.at[0, 0, 0], sib).wait_recv()

    def drain_gather(k):
        own(k, finish)
        for d in range(1, L):
            forward(k, d, finish, False)

    def normalize(k, _):
        rows = pl.ds(pl.multiple_of(k * rk, rk), rk)
        v = xt[rows, :].astype(jnp.float32) * scale * gcol[rows, :1]
        ga[k, f] = v.astype(jnp.bfloat16)

        @pl.when(k <= LEAD)
        def _():
            own(k, start)

        return 0

    lax.fori_loop(0, NC, normalize, 0)
    for k in range(LEAD):
        for d in range(1, L):
            forward(k, d, start, True)
    cot_copy.wait()

    def slab_at(c, place):
        found = jnp.int32(0)
        for s in range(1, G):
            found = jnp.where(owners[c, s] == place, s, found)
        return found

    def order(h):
        return list(range(nb)) if h == 0 else list(range(nb))[::-1]

    def place_of(h, i, flip, j):
        bits = order(h)
        place = jnp.int32(0)
        for m in range(i + 1):
            mine = bit(bits[m])
            place = place + (1 - mine if (flip and m == i) else mine) * (1 << bits[m])
        left = bits[i + 1:]
        for m, b in enumerate(left):
            place = place + ((j // (1 << (len(left) - 1 - m))) % 2) * (1 << b)
        return place

    def exchange(k, h, i):
        return remote(sends[i].at[k % 2, h], recvs[i].at[k, h], rs_send.at[i, k % 2, h], rs_recv.at[i, k, h],
                      (partner(order(h)[i]), f))

    def reuse(k, h, i):
        @pl.when(k >= 2)
        def _():
            exchange(k - 2, h, i).wait_send()

    def segments(h):
        for n in range(Nh // W):
            yield (h * Nh + n * W) // BLK, h * Nh + n * W, n * W

    def first_send(k):
        for h in range(2):
            reuse(k, h, 0)
            for j in range(G // 2):
                place = place_of(h, 0, True, j)
                for c, col, at in segments(h):
                    sends[0][k % 2, h, j, :, at:at + W] = res[k % 2, slab_at(c, place), :, col:col + W]
            exchange(k, h, 0).start()

    def receive(k, i):
        for h in range(2):
            exchange(k, h, i).wait_recv()
            if i == nb - 1:
                for c, col, at in segments(h):
                    if i == 0:
                        v = res[k % 2, slab_at(c, g), :, col:col + W].astype(jnp.float32)
                    else:
                        v = curs[i - 1][h, 0, :, at:at + W]
                    v = (v + recvs[i][k, h, 0, :, at:at + W].astype(jnp.float32)).astype(jnp.bfloat16)
                    for m in range(q):
                        og[pl.ds(pl.multiple_of(m * S + k * rk, rk), rk), col:col + W] = v[m * rk:(m + 1) * rk]
                continue
            reuse(k, h, i + 1)
            count = 1 << (nb - i - 2)
            mine = bit(order(h)[i + 1])
            for keep in (0, 1):
                side = mine if keep else 1 - mine
                for j in range(count):
                    at_j = side * count + j
                    place = place_of(h, i, False, at_j)
                    for c, col, at in segments(h):
                        if i == 0:
                            v = res[k % 2, slab_at(c, place), :, col:col + W].astype(jnp.float32)
                        else:
                            v = curs[i - 1][h, at_j, :, at:at + W]
                        v = v + recvs[i][k, h, at_j, :, at:at + W].astype(jnp.float32)
                        if keep:
                            curs[i][h, j, :, at:at + W] = v
                        else:
                            sends[i + 1][k % 2, h, j, :, at:at + W] = v.astype(jnp.bfloat16)
                if not keep:
                    exchange(k, h, i + 1).start()

    def step(t, _):
        @pl.when(t < NC)
        def _():
            wait_sibling(t)

            @pl.when(t >= RING - 1 - LEAD)
            def _():
                drain_gather(t + LEAD + 1 - RING)

            @pl.when(t + LEAD < NC)
            def _():
                forward(t + LEAD, 1, start, True)

            def tile(n, _):
                cols = pl.ds(pl.multiple_of(n * TN, TN), TN)
                v = jnp.dot(ga[t].reshape(M, T), cotv[:, cols], preferred_element_type=jnp.float32)
                res[t % 2, :, :, cols] = v.astype(jnp.bfloat16).reshape(G, R, TN)
                return 0

            lax.fori_loop(0, N // TN, tile, 0)
            first_send(t)

        for i in range(nb - 1, -1, -1):
            @pl.when((t - 1 - i >= 0) & (t - 1 - i < NC))
            def _():
                receive(t - 1 - i, i)

        @pl.when(t + LEAD < NC)
        def _():
            for d in range(2, L):
                forward(t + LEAD, d, start, True)

        @pl.when(t + LEAD + 1 < NC)
        def _():
            own(t + LEAD + 1, start)

        return 0

    lax.fori_loop(0, NC + nb, step, 0)
    for d in range(1, F):
        ss_copy(f, (f + d) % F, d).wait_send()
    for k in range(NC + LEAD + 1 - RING, NC):
        drain_gather(k)
    for i in range(nb):
        for h in range(2):
            for k in (NC - 2, NC - 1):
                exchange(k, h, i).wait_send()


def gradient(G, F, owners, gain, x, cot, NC=8, LEAD=1, TN=1024):
    NC = min(NC, x.shape[1] // 16)
    TN = min(TN, cot.shape[1])
    T, S = x.shape
    N = cot.shape[1]
    nb = G.bit_length() - 1
    L, q, rk, Nh = F // 2, F // G, S // NC, N // 2
    R = q * rk
    slab = S * F // G
    bf, f32 = jnp.bfloat16, jnp.float32
    counts = [G >> (i + 1) for i in range(nb)]
    dma = pltpu.SemaphoreType.DMA
    return pl.pallas_call(
        functools.partial(grad_kernel, G, F, NC, LEAD, TN),
        out_shape=jax.ShapeDtypeStruct((slab, N), bf),
        in_specs=[
            pl.BlockSpec(memory_space=pltpu.SMEM),
            pl.BlockSpec(memory_space=pltpu.VMEM),
            pl.BlockSpec(memory_space=pl.ANY),
            pl.BlockSpec(memory_space=pl.ANY),
        ],
        out_specs=pl.BlockSpec(memory_space=pltpu.VMEM),
        scratch_shapes=[
            pltpu.VMEM((T, S), bf),
            pltpu.VMEM((S, T), bf),
            pltpu.VMEM((S, 128), f32),
            pltpu.VMEM((T, N), bf),
            pltpu.VMEM((NC, F, rk, T), bf),
            pltpu.VMEM((F, 1, T), f32),
            pltpu.VMEM((2, G, R, N), bf),
        ]
        + [pltpu.VMEM((2, 2, n, R, Nh), bf) for n in counts]
        + [pltpu.VMEM((NC, 2, n, R, Nh), bf) for n in counts]
        + [pltpu.VMEM((2, n, R, Nh), f32) for n in counts[1:]]
        + [
            dma((2,)),
            dma((F - 1,)),
            dma((F,)),
            dma((RING, L, 2)),
            dma((RING,)),
            dma((NC, F)),
            dma((nb, 2, 2)),
            dma((nb, NC, 2)),
        ],
        compiler_params=pltpu.CompilerParams(
            collective_id=0, has_side_effects=True, vmem_limit_bytes=62 * 1024 * 1024
        ),
        cost_estimate=pl.CostEstimate(flops=2 * T * S * F * N, bytes_accessed=2 * (T * S + T * N + slab * N), transcendentals=0),
        name="gradient_step",
    )(owners, gain.reshape(1, S), x, cot)


SCALE_EPSILON = 1e-06
DECAY_RATE = 0.95
RIDGE_TERM = 1e-06
C0 = 1.5625
C1 = -0.3125 - 3125.0 / 4096.0
C2 = 3125.0 / 4096.0
C3 = -1250.0 / 4096.0
C4 = 250.0 / 4096.0
C5 = -25.0 / 4096.0
C6 = 1.0 / 4096.0


def dot(a, b, dims=(((1,), (0,)), ((), ()))):
    return lax.dot_general(a, b, dims, preferred_element_type=jnp.float32)


def split(value):
    high = value.astype(jnp.bfloat16)
    return high, (value - high.astype(jnp.float32)).astype(jnp.bfloat16)


def inverse_fourth_root(statistic):
    rows = lax.broadcasted_iota(jnp.int32, statistic.shape, 0)
    cols = lax.broadcasted_iota(jnp.int32, statistic.shape, 1)
    diagonal = rows == cols
    matrix = statistic + jnp.where(diagonal, RIDGE_TERM, 0.0)
    scaling = 2.5 * lax.rsqrt(jnp.sum(matrix * matrix, keepdims=True))
    m1 = scaling * matrix
    m1_low = m1.astype(jnp.bfloat16)
    m2 = dot(m1_low, m1_low)
    m3 = dot(m2.astype(jnp.bfloat16), m1_low)
    upper = dot(
        m3.astype(jnp.bfloat16), (C4 * m1 + C5 * m2 + C6 * m3).astype(jnp.bfloat16)
    )
    total = C1 * m1 + C2 * m2 + C3 * m3 + upper + jnp.where(diagonal, C0, 0.0)
    return jnp.sqrt(jnp.sqrt(scaling)) * total


def condition_kernel(G, g_ref, li_ref, ri_ref, *rest):
    outs, held = rest[:G], rest[G]
    me = lax.axis_index("group")
    grad = g_ref[...]
    left_high, left_low = split(li_ref[...])
    half = dot(left_high, grad) + dot(left_low, grad)
    half_high, half_low = split(half)
    right_high, right_low = split(ri_ref[...])
    conditioned = dot(half_high, right_high) + dot(half_low, right_high) + dot(half_high, right_low)
    mean = jnp.sum(conditioned * conditioned, keepdims=True) * (1.0 / conditioned.size)
    held[...] = (conditioned * lax.rsqrt(mean + SCALE_EPSILON)).astype(jnp.bfloat16)
    rows = BLK // G
    for m in range(G):
        outs[m][...] = held[pl.ds(pl.multiple_of((me ^ m) * rows, rows), rows), :]


def condition(G, r, grad, left, right):
    N = grad.shape[1]
    here = pl.BlockSpec((BLK, BLK), lambda c: (r, c))
    part = pl.BlockSpec((BLK // G, BLK), lambda c: (0, c))
    return pl.pallas_call(
        functools.partial(condition_kernel, G),
        grid=(N // BLK,),
        in_specs=[here] * 3,
        out_specs=[part] * G,
        out_shape=[jax.ShapeDtypeStruct((BLK // G, N), jnp.bfloat16)] * G,
        scratch_shapes=[pltpu.VMEM((BLK, BLK), jnp.bfloat16)],
        compiler_params=pltpu.CompilerParams(
            dimension_semantics=("arbitrary",), vmem_limit_bytes=40 * 1024 * 1024
        ),
        cost_estimate=pl.CostEstimate(
            flops=(N // BLK) * 5 * 2 * BLK**3, bytes_accessed=(N // BLK) * 12 * BLK * BLK, transcendentals=0
        ),
        name="condition_step",
    )(grad, left, right)


def stats_kernel(r, col_blocks, refresh, g_ref, ls_ref, rs_ref, li_ref, ri_ref, *rest):
    la_ref, ra_ref, ln_ref, rn_ref = rest[-4:]
    grad = g_ref[...]
    la_ref[...] = DECAY_RATE * ls_ref[...] + (1.0 - DECAY_RATE) * dot(
        grad, grad, (((1,), (1,)), ((), ()))
    )
    ra_ref[...] = DECAY_RATE * rs_ref[...] + (1.0 - DECAY_RATE) * dot(
        grad, grad, (((0,), (0,)), ((), ()))
    )
    flag = refresh[r * col_blocks + pl.program_id(0)]

    @pl.when(flag > 0)
    def _():
        ln_ref[...] = inverse_fourth_root(la_ref[...])
        rn_ref[...] = inverse_fourth_root(ra_ref[...])

    @pl.when(flag <= 0)
    def _():
        ln_ref[...] = li_ref[...]
        rn_ref[...] = ri_ref[...]


def stats(r, grad, refresh, states, previous):
    slab_rows, N = states[0].shape
    col_blocks = N // BLK
    here = pl.BlockSpec((BLK, BLK), lambda c, flags: (r, c))
    held = [pl.BlockSpec(memory_space=pl.ANY)] * len(previous)
    whole = jax.ShapeDtypeStruct((slab_rows, N), jnp.float32)
    return pl.pallas_call(
        functools.partial(stats_kernel, r, col_blocks),
        grid_spec=pltpu.PrefetchScalarGridSpec(
            num_scalar_prefetch=1,
            grid=(col_blocks,),
            in_specs=[here] * 5 + held,
            out_specs=[here] * 4,
        ),
        out_shape=[whole] * 4,
        input_output_aliases={6 + i: i for i in range(len(previous))},
        compiler_params=pltpu.CompilerParams(
            dimension_semantics=("arbitrary",), vmem_limit_bytes=48 * 1024 * 1024
        ),
        cost_estimate=pl.CostEstimate(
            flops=col_blocks * 8 * 2 * BLK**3,
            bytes_accessed=col_blocks * 9 * 4 * BLK * BLK,
            transcendentals=0,
        ),
        name="stats_step",
    )(refresh, grad, *states, *previous)


def relay_kernel(G, owners, *refs):
    ins, outs = refs[:G], refs[G:]
    me = lax.axis_index("group")
    c = pl.program_id(0)
    for m in range(G):
        wanted = owners[c * G + (me ^ m)] ^ me
        for k in range(G):
            @pl.when(wanted == k)
            def _():
                outs[m][...] = ins[k][...]


def relay(G, owners, parts):
    rows, N = parts[0].shape
    part = pl.BlockSpec((rows, BLK), lambda c, own: (0, c))
    return pl.pallas_call(
        functools.partial(relay_kernel, G),
        grid_spec=pltpu.PrefetchScalarGridSpec(
            num_scalar_prefetch=1, grid=(N // BLK,), in_specs=[part] * G, out_specs=[part] * G
        ),
        out_shape=[jax.ShapeDtypeStruct((rows, N), jnp.bfloat16)] * G,
        compiler_params=pltpu.CompilerParams(dimension_semantics=("arbitrary",)),
        cost_estimate=pl.CostEstimate(flops=0, bytes_accessed=4 * G * rows * N, transcendentals=0),
        name="relay_step",
    )(owners, *parts)


def place_kernel(G, *refs):
    ins, out = refs[:G], refs[-1]
    me = lax.axis_index("group")
    rows = BLK // G
    for m in range(G):
        out[pl.ds(pl.multiple_of((me ^ m) * rows, rows), rows), :] = ins[m][...]


def place(G, r, slab_rows, parts, previous):
    rows, N = parts[0].shape
    part = pl.BlockSpec((rows, BLK), lambda c: (0, c))
    return pl.pallas_call(
        functools.partial(place_kernel, G),
        grid=(N // BLK,),
        in_specs=[part] * G + [pl.BlockSpec(memory_space=pl.ANY)] * len(previous),
        out_specs=pl.BlockSpec((BLK, BLK), lambda c: (r, c)),
        out_shape=jax.ShapeDtypeStruct((slab_rows, N), jnp.bfloat16),
        input_output_aliases={G: 0} if previous else {},
        compiler_params=pltpu.CompilerParams(dimension_semantics=("arbitrary",)),
        cost_estimate=pl.CostEstimate(flops=0, bytes_accessed=4 * BLK * N, transcendentals=0),
        name="place_step",
    )(*parts, *previous)


def swap(G, parts):
    return [parts[0]] + [
        lax.ppermute(parts[m], "group", [(i, i ^ m) for i in range(G)]) for m in range(1, G)
    ]


def body(G, F, inputs, norm_gain, cotangent, owners, refresh, *states):
    slab_rows, N = states[0].shape
    own = gradient(G, F, owners, norm_gain, inputs, cotangent)
    flat_owners = owners.reshape(-1)
    count = slab_rows // BLK
    sent = [swap(G, condition(G, r, own, states[2], states[3])) for r in range(count)]
    previous = ()
    back = []
    for r in range(count):
        previous = tuple(stats(r, own, refresh.reshape(-1), states, previous))
        back.append(swap(G, relay(G, flat_owners, sent[r])))
    update = ()
    for r in range(count):
        update = (place(G, r, slab_rows, back[r], update),)
    return (*update, *previous)


def solution(mesh):
    spec = P("group", "fsdp")
    in_specs = (spec, P("fsdp"), spec, P("fsdp", None), spec, spec, spec, spec, spec)
    return jax.shard_map(
        functools.partial(body, mesh.shape["group"], mesh.shape["fsdp"]),
        mesh=mesh, in_specs=in_specs, out_specs=(spec,) * 5, check_vma=False
    )
```

```python
import functools
import jax
import jax.numpy as jnp
from jax import lax
from jax.experimental import pallas as pl
from jax.experimental.pallas import tpu as pltpu
from jax.sharding import PartitionSpec as P


BLK = 512
ANY = pl.BlockSpec(memory_space=pl.ANY)
VMEM_LIMIT = 62 * 1024 * 1024
NORM_EPSILON = 1e-05
MESH = pl.DeviceIdType.MESH
RING = 8


def remote(src, dst, send_sem, recv_sem, device):
    return pltpu.make_async_remote_copy(
        src_ref=src, dst_ref=dst, send_sem=send_sem, recv_sem=recv_sem,
        device_id=device, device_id_type=MESH,
    )


def grad_kernel(G, F, NC, LAG, LEAD, owners, gain, x_hbm, cot_hbm, og, xbuf, gcol, scol, cotv, ga, ssall, res, *rest):
    nb = G.bit_length() - 1
    sends, recvs, curs = rest[:nb], rest[nb:2 * nb], rest[2 * nb:3 * nb - 1]
    lsem, ss_send, ss_recv, go, gf, gr, rs_send, rs_recv = rest[3 * nb - 1:]
    T, S = xbuf.shape
    N = cotv.shape[1]
    D = S * F
    L, q, rk, Nh = F // 2, F // G, S // NC, N // 2
    R, M = q * rk, F * rk
    W = min(BLK, Nh)
    g, f = lax.axis_index("group"), lax.axis_index("fsdp")
    l, core = f // 2, f % 2
    sib = f + 1 - 2 * core

    def bit(b):
        return (g // (1 << b)) % 2

    def partner(b):
        return g + (1 - 2 * bit(b)) * (1 << b)

    x_copy = pltpu.make_async_copy(x_hbm, xbuf, lsem.at[0])
    x_copy.start()
    cot_copy = pltpu.make_async_copy(cot_hbm, cotv, lsem.at[1])
    cot_copy.start()

    barrier = pltpu.get_barrier_semaphore()
    for d in range(1, F):
        pl.semaphore_signal(barrier, inc=1, device_id=(g, (f + d) % F), device_id_type=MESH)
    for b in range(nb):
        pl.semaphore_signal(barrier, inc=1, device_id=(partner(b), f), device_id_type=MESH)

    gcol[...] = jnp.broadcast_to(gain[...].astype(jnp.float32), (128, S)).T
    x_copy.wait()
    TT = 256
    for i in range(T // TT):
        at = slice(i * TT, (i + 1) * TT)
        v = xbuf[at, :].astype(jnp.float32).T
        ssall[f, :, at] = jnp.sum(v * v, axis=0, keepdims=True)
        v = (v * gcol[:, :1]).astype(jnp.bfloat16)
        for k in range(NC):
            ga[k, f, :, at] = v[k * rk:(k + 1) * rk]
    pl.semaphore_wait(barrier, F - 1 + nb)

    def ss_copy(slot, peer, d):
        return remote(ssall.at[slot], ssall.at[slot], ss_send.at[d - 1], ss_recv.at[slot], (g, peer))

    def piece(k, shard, send_sem, peer):
        return remote(ga.at[k, shard], ga.at[k, shard], send_sem, gr.at[k, shard], (g, peer))

    def pass_on(k, src, sems, sides, then):
        shard = 2 * src + core
        for m, side in enumerate(sides):
            for hop in (1, 2):
                peer = l + side * hop

                @pl.when((peer >= 0) & (peer <= L - 1))
                def _():
                    then(piece(k, shard, sems.at[2 * m + hop - 1], f + 2 * side * hop))

        then(piece(k, shard, sems.at[2 * len(sides)], sib))

    def own(k, then):
        pass_on(k, l, go.at[k % RING], (1, -1), then)

    def forward(k, d, then, receive):
        for side in (1, -1):
            src = l - side * d

            @pl.when((src >= 0) & (src <= L - 1))
            def _():
                if receive:
                    piece(k, 2 * src + core, go.at[0, 0], sib).wait_recv()
                pass_on(k, src, gf.at[k % 4, src], (side,) if d % 2 == 0 else (), then)

    def start(copy):
        copy.start()

    def finish(copy):
        copy.wait_send()

    def wait_sibling(k):
        for src in range(L):
            piece(k, 2 * src + 1 - core, go.at[0, 0], sib).wait_recv()

    def drain_gather(k):
        own(k, finish)
        for d in range(1, L):
            forward(k, d, finish, False)

    for d in range(1, F):
        ss_copy(f, (f + d) % F, d).start()
    own(0, start)
    own(1, start)
    for d in range(1, F):
        peer = (f + d) % F
        ss_copy(peer, peer, d).wait_recv()
    scale = lax.rsqrt(jnp.sum(ssall[...], axis=0) * (1.0 / D) + NORM_EPSILON)
    scol[...] = jnp.broadcast_to(scale, (128, T)).T
    cot_copy.wait()

    def scale_cotangent(i, _):
        rows = pl.ds(pl.multiple_of(i * 256, 256), 256)
        cotv[rows, :] = (cotv[rows, :].astype(jnp.float32) * scol[rows, :1]).astype(jnp.bfloat16)
        return 0

    def forward_all(k):
        for d in range(1, L):
            forward(k, d, start, True)

    lax.fori_loop(0, T // 256, scale_cotangent, 0)
    forward_all(0)
    for k in range(2, min(LEAD, NC)):
        own(k, start)
    ends = (l == 0) | (l == L - 1)

    def slab_at(c, place):
        found = jnp.int32(0)
        for s in range(1, G):
            found = jnp.where(owners[c, s] == place, s, found)
        return found

    def order(h):
        return list(range(nb)) if h == 0 else list(range(nb))[::-1]

    def place_of(h, i, flip, j):
        bits = order(h)
        place = jnp.int32(0)
        for m in range(i + 1):
            mine = bit(bits[m])
            place = place + (1 - mine if (flip and m == i) else mine) * (1 << bits[m])
        left = bits[i + 1:]
        for m, b in enumerate(left):
            place = place + ((j // (1 << (len(left) - 1 - m))) % 2) * (1 << b)
        return place

    def exchange(k, h, i):
        return remote(sends[i].at[k % 2, h], recvs[i].at[k, h], rs_send.at[i, k % 2, h], rs_recv.at[i, k, h],
                      (partner(order(h)[i]), f))

    def reuse(k, h, i):
        @pl.when(k >= 2)
        def _():
            exchange(k - 2, h, i).wait_send()

    def segments(h):
        for n in range(Nh // W):
            yield (h * Nh + n * W) // BLK, h * Nh + n * W, n * W

    def first_send(k, h):
        reuse(k, h, 0)
        for j in range(G // 2):
            place = place_of(h, 0, True, j)
            for c, col, at in segments(h):
                sends[0][k % 2, h, j, :, at:at + W] = res[k % (LAG + 1), slab_at(c, place), :, col:col + W]
        exchange(k, h, 0).start()

    def receive(k, i):
        for h in range(2):
            exchange(k, h, i).wait_recv()
            if i == nb - 1:
                for c, col, at in segments(h):
                    if i == 0:
                        v = res[k % (LAG + 1), slab_at(c, g), :, col:col + W].astype(jnp.float32)
                    else:
                        v = curs[i - 1][k % LAG, h, 0, :, at:at + W]
                    v = (v + recvs[i][k, h, 0, :, at:at + W].astype(jnp.float32)).astype(jnp.bfloat16)
                    for m in range(q):
                        og[pl.ds(pl.multiple_of(m * S + k * rk, rk), rk), col:col + W] = v[m * rk:(m + 1) * rk]
                continue
            reuse(k, h, i + 1)
            count = 1 << (nb - i - 2)
            mine = bit(order(h)[i + 1])
            for keep in (0, 1):
                side = mine if keep else 1 - mine
                for j in range(count):
                    at_j = side * count + j
                    place = place_of(h, i, False, at_j)
                    for c, col, at in segments(h):
                        if i == 0:
                            v = res[k % (LAG + 1), slab_at(c, place), :, col:col + W].astype(jnp.float32)
                        else:
                            v = curs[i - 1][k % LAG, h, at_j, :, at:at + W]
                        v = v + recvs[i][k, h, at_j, :, at:at + W].astype(jnp.float32)
                        if keep:
                            curs[i][k % LAG, h, j, :, at:at + W] = v
                        else:
                            sends[i + 1][k % 2, h, j, :, at:at + W] = v.astype(jnp.bfloat16)
                if not keep:
                    exchange(k, h, i + 1).start()

    def step(t, _):
        ahead = t + 1 < NC

        @pl.when(t < NC)
        def _():
            wait_sibling(t)

            @pl.when(t >= 2)
            def _():
                drain_gather(t - 2)

            @pl.when(ahead & jnp.logical_not(ends))
            def _():
                forward(t + 1, 1, start, True)

            for h in range(2):
                cols = slice(h * Nh, (h + 1) * Nh)
                v = jnp.dot(ga[t].reshape(M, T), cotv[:, cols], preferred_element_type=jnp.float32)
                res[t % (LAG + 1), :, :, cols] = v.astype(jnp.bfloat16).reshape(G, R, Nh)
                first_send(t, h)

            @pl.when(ahead & ends)
            def _():
                forward(t + 1, 1, start, True)

            @pl.when(ahead)
            def _():
                forward(t + 1, 2, start, True)

        for i in range(nb - 1, -1, -1):
            k = t - LAG * (i + 1)

            @pl.when((k >= 0) & (k < NC))
            def _():
                receive(k, i)

        @pl.when(ahead)
        def _():
            for d in range(3, L):
                forward(t + 1, d, start, True)

        @pl.when(t + LEAD < NC)
        def _():
            own(t + LEAD, start)

        return 0

    lax.fori_loop(0, NC + nb * LAG, step, 0)
    for d in range(1, F):
        ss_copy(f, (f + d) % F, d).wait_send()
    for k in range(NC - 2, NC):
        drain_gather(k)
    for i in range(nb):
        for h in range(2):
            for k in (NC - 2, NC - 1):
                exchange(k, h, i).wait_send()


def gradient(G, F, owners, gain, x, cot, NC=16, LAG=1, LEAD=3):
    NC = min(NC, x.shape[1] // 16)
    T, S = x.shape
    N = cot.shape[1]
    nb = G.bit_length() - 1
    L, q, rk, Nh = F // 2, F // G, S // NC, N // 2
    R = q * rk
    slab = S * F // G
    bf, f32 = jnp.bfloat16, jnp.float32
    counts = [G >> (i + 1) for i in range(nb)]
    dma = pltpu.SemaphoreType.DMA
    return pl.pallas_call(
        functools.partial(grad_kernel, G, F, NC, LAG, LEAD),
        out_shape=jax.ShapeDtypeStruct((slab, N), bf),
        in_specs=[
            pl.BlockSpec(memory_space=pltpu.SMEM),
            pl.BlockSpec(memory_space=pltpu.VMEM),
            pl.BlockSpec(memory_space=pl.ANY),
            pl.BlockSpec(memory_space=pl.ANY),
        ],
        out_specs=pl.BlockSpec(memory_space=pltpu.VMEM),
        scratch_shapes=[
            pltpu.VMEM((T, S), bf),
            pltpu.VMEM((S, 128), f32),
            pltpu.VMEM((T, 128), f32),
            pltpu.VMEM((T, N), bf),
            pltpu.VMEM((NC, F, rk, T), bf),
            pltpu.VMEM((F, 1, T), f32),
            pltpu.VMEM((LAG + 1, G, R, N), bf),
        ]
        + [pltpu.VMEM((2, 2, n, R, Nh), bf) for n in counts]
        + [pltpu.VMEM((NC, 2, n, R, Nh), bf) for n in counts]
        + [pltpu.VMEM((LAG, 2, n, R, Nh), f32) for n in counts[1:]]
        + [
            dma((2,)),
            dma((F - 1,)),
            dma((F,)),
            dma((RING, 5)),
            dma((4, L, 3)),
            dma((NC, F)),
            dma((nb, 2, 2)),
            dma((nb, NC, 2)),
        ],
        compiler_params=pltpu.CompilerParams(
            collective_id=0, has_side_effects=True, vmem_limit_bytes=VMEM_LIMIT
        ),
        cost_estimate=pl.CostEstimate(flops=2 * T * S * F * N, bytes_accessed=2 * (T * S + T * N + slab * N), transcendentals=0),
        name="gradient_step",
    )(owners, gain.reshape(1, S), x, cot)


SCALE_EPSILON = 1e-06
DECAY_RATE = 0.95
RIDGE_TERM = 1e-06
C0 = 1.5625
C1 = -0.3125 - 3125.0 / 4096.0
C2 = 3125.0 / 4096.0
C3 = -1250.0 / 4096.0
C4 = 250.0 / 4096.0
C5 = -25.0 / 4096.0
C6 = 1.0 / 4096.0


def dot(a, b, dims=(((1,), (0,)), ((), ()))):
    return lax.dot_general(a, b, dims, preferred_element_type=jnp.float32)


def split(value):
    high = value.astype(jnp.bfloat16)
    return high, (value - high.astype(jnp.float32)).astype(jnp.bfloat16)


def inverse_fourth_root(statistic):
    rows = lax.broadcasted_iota(jnp.int32, statistic.shape, 0)
    cols = lax.broadcasted_iota(jnp.int32, statistic.shape, 1)
    diagonal = rows == cols
    matrix = statistic + jnp.where(diagonal, RIDGE_TERM, 0.0)
    scaling = 2.5 * lax.rsqrt(jnp.sum(matrix * matrix, keepdims=True))
    m1 = scaling * matrix
    m1_low = m1.astype(jnp.bfloat16)
    m2 = dot(m1_low, m1_low)
    m3 = dot(m2.astype(jnp.bfloat16), m1_low)
    upper = dot(
        m3.astype(jnp.bfloat16), (C4 * m1 + C5 * m2 + C6 * m3).astype(jnp.bfloat16)
    )
    total = C1 * m1 + C2 * m2 + C3 * m3 + upper + jnp.where(diagonal, C0, 0.0)
    return jnp.sqrt(jnp.sqrt(scaling)) * total


def condition_kernel(G, g_ref, li_ref, ri_ref, *rest):
    outs, held = rest[-G - 1:-1], rest[-1]
    me = lax.axis_index("group")
    grad = g_ref[...]
    left_high, left_low = split(li_ref[...])
    half = dot(left_high, grad) + dot(left_low, grad)
    half_high, half_low = split(half)
    right_high, right_low = split(ri_ref[...])
    conditioned = dot(half_high, right_high) + dot(half_low, right_high) + dot(half_high, right_low)
    mean = jnp.sum(conditioned * conditioned, keepdims=True) * (1.0 / conditioned.size)
    held[...] = (conditioned * lax.rsqrt(mean + SCALE_EPSILON)).astype(jnp.bfloat16)
    rows = BLK // G
    for m in range(G):
        outs[m][...] = held[pl.ds(pl.multiple_of((me ^ m) * rows, rows), rows), :]


def condition(G, unit, grad, left, right, after):
    r, first, count = unit
    N = count * BLK
    here = pl.BlockSpec((BLK, BLK), lambda c: (r, first + c))
    part = pl.BlockSpec((BLK // G, BLK), lambda c: (0, c))
    return pl.pallas_call(
        functools.partial(condition_kernel, G),
        grid=(N // BLK,),
        in_specs=[here] * 3 + [ANY] * len(after),
        out_specs=[part] * G,
        out_shape=[jax.ShapeDtypeStruct((BLK // G, N), jnp.bfloat16)] * G,
        scratch_shapes=[pltpu.VMEM((BLK, BLK), jnp.bfloat16)],
        compiler_params=pltpu.CompilerParams(
            dimension_semantics=("arbitrary",), vmem_limit_bytes=VMEM_LIMIT
        ),
        cost_estimate=pl.CostEstimate(
            flops=(N // BLK) * 5 * 2 * BLK**3, bytes_accessed=(N // BLK) * 12 * BLK * BLK, transcendentals=0
        ),
        name="condition_step",
    )(grad, left, right, *after)


def stats_kernel(r, col_blocks, refresh, g_ref, ls_ref, rs_ref, li_ref, ri_ref, *rest):
    la_ref, ra_ref, ln_ref, rn_ref, token = rest[-5:]
    token[...] = jnp.zeros_like(token)
    grad = g_ref[...]
    la_ref[...] = DECAY_RATE * ls_ref[...] + (1.0 - DECAY_RATE) * dot(
        grad, grad, (((1,), (1,)), ((), ()))
    )
    ra_ref[...] = DECAY_RATE * rs_ref[...] + (1.0 - DECAY_RATE) * dot(
        grad, grad, (((0,), (0,)), ((), ()))
    )
    flag = refresh[r * col_blocks + pl.program_id(0)]

    @pl.when(flag > 0)
    def _():
        ln_ref[...] = inverse_fourth_root(la_ref[...])
        rn_ref[...] = inverse_fourth_root(ra_ref[...])

    @pl.when(flag <= 0)
    def _():
        ln_ref[...] = li_ref[...]
        rn_ref[...] = ri_ref[...]


def stats(r, grad, refresh, states, previous, after):
    slab_rows, N = states[0].shape
    col_blocks = N // BLK
    here = pl.BlockSpec((BLK, BLK), lambda c, flags: (r, c))
    held = [ANY] * (len(previous) + len(after))
    whole = jax.ShapeDtypeStruct((slab_rows, N), jnp.float32)
    return pl.pallas_call(
        functools.partial(stats_kernel, r, col_blocks),
        grid_spec=pltpu.PrefetchScalarGridSpec(
            num_scalar_prefetch=1,
            grid=(col_blocks,),
            in_specs=[here] * 5 + held,
            out_specs=[here] * 4 + [pl.BlockSpec((8, 128), lambda c, flags: (0, 0))],
        ),
        out_shape=[whole] * 4 + [jax.ShapeDtypeStruct((8, 128), jnp.float32)],
        input_output_aliases={6 + i: i for i in range(len(previous))},
        compiler_params=pltpu.CompilerParams(
            dimension_semantics=("arbitrary",), vmem_limit_bytes=VMEM_LIMIT
        ),
        cost_estimate=pl.CostEstimate(
            flops=col_blocks * 8 * 2 * BLK**3,
            bytes_accessed=col_blocks * 9 * 4 * BLK * BLK,
            transcendentals=0,
        ),
        name="stats_step",
    )(refresh, grad, *states, *previous, *after)


def relay_kernel(G, first, owners, *refs):
    ins, outs = refs[:G], refs[-G:]
    me = lax.axis_index("group")
    c = first + pl.program_id(0)
    for m in range(G):
        wanted = owners[c * G + (me ^ m)] ^ me
        for k in range(G):
            @pl.when(wanted == k)
            def _():
                outs[m][...] = ins[k][...]


def relay(G, unit, owners, parts, after):
    rows, N = parts[0].shape
    part = pl.BlockSpec((rows, BLK), lambda c, own: (0, c))
    return pl.pallas_call(
        functools.partial(relay_kernel, G, unit[1]),
        grid_spec=pltpu.PrefetchScalarGridSpec(
            num_scalar_prefetch=1, grid=(N // BLK,), in_specs=[part] * G + [ANY] * len(after), out_specs=[part] * G
        ),
        out_shape=[jax.ShapeDtypeStruct((rows, N), jnp.bfloat16)] * G,
        compiler_params=pltpu.CompilerParams(
            dimension_semantics=("arbitrary",), vmem_limit_bytes=VMEM_LIMIT
        ),
        cost_estimate=pl.CostEstimate(flops=0, bytes_accessed=4 * G * rows * N, transcendentals=0),
        name="relay_step",
    )(owners, *parts, *after)


def place_kernel(G, *refs):
    ins, out = refs[:G], refs[-1]
    me = lax.axis_index("group")
    rows = BLK // G
    for m in range(G):
        out[pl.ds(pl.multiple_of((me ^ m) * rows, rows), rows), :] = ins[m][...]


def place(G, unit, shape, parts, previous, after):
    rows, N = parts[0].shape
    r, first = unit[:2]
    part = pl.BlockSpec((rows, BLK), lambda c: (0, c))
    return pl.pallas_call(
        functools.partial(place_kernel, G),
        grid=(N // BLK,),
        in_specs=[part] * G + [ANY] * (len(previous) + len(after)),
        out_specs=pl.BlockSpec((BLK, BLK), lambda c: (r, first + c)),
        out_shape=jax.ShapeDtypeStruct(shape, jnp.bfloat16),
        input_output_aliases={G: 0} if previous else {},
        compiler_params=pltpu.CompilerParams(
            dimension_semantics=("arbitrary",), vmem_limit_bytes=VMEM_LIMIT
        ),
        cost_estimate=pl.CostEstimate(flops=0, bytes_accessed=4 * BLK * N, transcendentals=0),
        name="place_step",
    )(*parts, *previous, *after)


def swap(G, parts):
    out = [parts[0]]
    for m in range(1, G):
        out.append(lax.ppermute(parts[m], "group", [(i, i ^ m) for i in range(G)]))
    return out


def cut(count, blocks):
    units = []
    for r in range(count):
        cuts = [0, 1, blocks] if r == 0 and blocks > 1 else [0, blocks]
        units += [(r, lo, hi - lo) for lo, hi in zip(cuts, cuts[1:])]
    return units


def body(G, F, inputs, norm_gain, cotangent, owners, refresh, *states):
    slab_rows, N = states[0].shape
    own = gradient(G, F, owners, norm_gain, inputs, cotangent)
    flat_owners = owners.reshape(-1)
    count, blocks = slab_rows // BLK, N // BLK
    units = cut(count, blocks)
    sent, back, after = [], [], ()
    for unit in units:
        parts = condition(G, unit, own, states[2], states[3], after)
        after = (parts[0],)
        sent.append(swap(G, parts))
    previous = ()
    for r in range(count):
        *previous, token = stats(r, own, refresh.reshape(-1), states, tuple(previous), after)
        after = (token,)
        if r == 0:
            for unit, parts in zip(units, sent):
                parts = relay(G, unit, flat_owners, parts, after)
                after = (parts[0],)
                back.append(swap(G, parts))
    update = ()
    for unit, parts in zip(units, back):
        update = (place(G, unit, (slab_rows, N), parts, update, after),)
    return (*update, *previous)


def solution(mesh):
    spec = P("group", "fsdp")
    in_specs = (spec, P("fsdp"), spec, P("fsdp", None), spec, spec, spec, spec, spec)
    G, F = mesh.shape["group"], mesh.shape["fsdp"]

    def whole(*args):
        def local(*blocks_of):
            return body(G, F, *blocks_of)

        step = jax.shard_map(
            local, mesh=mesh, in_specs=in_specs, out_specs=(spec,) * 5, check_vma=False
        )
        return step(*args)

    return whole
```

```python
import functools
import jax
import jax.numpy as jnp
from jax import lax
from jax.experimental import pallas as pl
from jax.experimental.pallas import tpu as pltpu
from jax.sharding import PartitionSpec as P


BLK = 512
ANY = pl.BlockSpec(memory_space=pl.ANY)
VMEM_LIMIT = 62 * 1024 * 1024
NORM_EPSILON = 1e-05
MESH = pl.DeviceIdType.MESH
RING = 8


def remote(src, dst, send_sem, recv_sem, device):
    return pltpu.make_async_remote_copy(
        src_ref=src, dst_ref=dst, send_sem=send_sem, recv_sem=recv_sem,
        device_id=device, device_id_type=MESH,
    )


def grad_kernel(G, F, NC, LAG, LEAD, owners, gain, x_hbm, cot_hbm, out, og, xbuf, gcol, scol, cotv, ga, ssall, res, *rest):
    nb = G.bit_length() - 1
    sends, recvs, curs = rest[:nb], rest[nb:2 * nb], rest[2 * nb:3 * nb - 1]
    lsem, out_sem, ss_send, ss_recv, go, gf, gr, rs_send, rs_recv = rest[3 * nb - 1:]
    T, S = xbuf.shape
    N = cotv.shape[1]
    D = S * F
    L, q, rk, Nh = F // 2, F // G, S // NC, N // 2
    R, M = q * rk, F * rk
    W = min(BLK, Nh)
    g, f = lax.axis_index("group"), lax.axis_index("fsdp")
    l, core = f // 2, f % 2
    sib = f + 1 - 2 * core

    def bit(b):
        return (g // (1 << b)) % 2

    def partner(b):
        return g + (1 - 2 * bit(b)) * (1 << b)

    x_copy = pltpu.make_async_copy(x_hbm, xbuf, lsem.at[0])
    x_copy.start()
    cot_copy = pltpu.make_async_copy(cot_hbm, cotv, lsem.at[1])
    cot_copy.start()

    barrier = pltpu.get_barrier_semaphore()
    for d in range(1, F):
        pl.semaphore_signal(barrier, inc=1, device_id=(g, (f + d) % F), device_id_type=MESH)
    for b in range(nb):
        pl.semaphore_signal(barrier, inc=1, device_id=(partner(b), f), device_id_type=MESH)

    gcol[...] = jnp.broadcast_to(gain[...].astype(jnp.float32)[None, :], (128, S)).T
    x_copy.wait()
    TT = 256
    for i in range(T // TT):
        at = slice(i * TT, (i + 1) * TT)
        v = xbuf[at, :].astype(jnp.float32).T
        ssall[f, :, at] = jnp.sum(v * v, axis=0, keepdims=True)
        v = (v * gcol[:, :1]).astype(jnp.bfloat16)
        for k in range(NC):
            ga[k, f, :, at] = v[k * rk:(k + 1) * rk]
    pl.semaphore_wait(barrier, F - 1 + nb)

    def ss_copy(slot, peer, d):
        return remote(ssall.at[slot], ssall.at[slot], ss_send.at[d - 1], ss_recv.at[slot], (g, peer))

    def piece(k, shard, send_sem, peer):
        return remote(ga.at[k, shard], ga.at[k, shard], send_sem, gr.at[k, shard], (g, peer))

    def pass_on(k, src, sems, sides, then):
        shard = 2 * src + core
        for m, side in enumerate(sides):
            for hop in (1, 2):
                peer = l + side * hop

                @pl.when((peer >= 0) & (peer <= L - 1))
                def _():
                    then(piece(k, shard, sems.at[2 * m + hop - 1], f + 2 * side * hop))

        then(piece(k, shard, sems.at[2 * len(sides)], sib))

    def own(k, then):
        pass_on(k, l, go.at[k % RING], (1, -1), then)

    def forward(k, d, then, receive):
        for side in (1, -1):
            src = l - side * d

            @pl.when((src >= 0) & (src <= L - 1))
            def _():
                if receive:
                    piece(k, 2 * src + core, go.at[0, 0], sib).wait_recv()
                pass_on(k, src, gf.at[k % 4, src], (side,) if d % 2 == 0 else (), then)

    def start(copy):
        copy.start()

    def finish(copy):
        copy.wait_send()

    def wait_sibling(k):
        for src in range(L):
            piece(k, 2 * src + 1 - core, go.at[0, 0], sib).wait_recv()

    def drain_gather(k):
        own(k, finish)
        for d in range(1, L):
            forward(k, d, finish, False)

    for d in range(1, F):
        ss_copy(f, (f + d) % F, d).start()
    own(0, start)
    own(1, start)
    for d in range(1, F):
        peer = (f + d) % F
        ss_copy(peer, peer, d).wait_recv()
    scale = lax.rsqrt(jnp.sum(ssall[...], axis=0) * (1.0 / D) + NORM_EPSILON)
    scol[...] = jnp.broadcast_to(scale, (128, T)).T
    cot_copy.wait()

    def scale_cotangent(i, _):
        rows = pl.ds(pl.multiple_of(i * 256, 256), 256)
        cotv[rows, :] = (cotv[rows, :].astype(jnp.float32) * scol[rows, :1]).astype(jnp.bfloat16)
        return 0

    def forward_all(k):
        for d in range(1, L):
            forward(k, d, start, True)

    lax.fori_loop(0, T // 256, scale_cotangent, 0)
    forward_all(0)
    for k in range(2, min(LEAD, NC)):
        own(k, start)
    ends = (l == 0) | (l == L - 1)

    def slab_at(c, place):
        found = jnp.int32(0)
        for s in range(1, G):
            found = jnp.where(owners[c, s] == place, s, found)
        return found

    def order(h):
        return list(range(nb)) if h == 0 else list(range(nb))[::-1]

    def place_of(h, i, flip, j):
        bits = order(h)
        place = jnp.int32(0)
        for m in range(i + 1):
            mine = bit(bits[m])
            place = place + (1 - mine if (flip and m == i) else mine) * (1 << bits[m])
        left = bits[i + 1:]
        for m, b in enumerate(left):
            place = place + ((j // (1 << (len(left) - 1 - m))) % 2) * (1 << b)
        return place

    def exchange(k, h, i):
        return remote(sends[i].at[k % 2, h], recvs[i].at[k, h], rs_send.at[i, k % 2, h], rs_recv.at[i, k, h],
                      (partner(order(h)[i]), f))

    def reuse(k, h, i):
        @pl.when(k >= 2)
        def _():
            exchange(k - 2, h, i).wait_send()

    def segments(h):
        for n in range(Nh // W):
            yield (h * Nh + n * W) // BLK, h * Nh + n * W, n * W

    def first_send(k, h):
        reuse(k, h, 0)
        for j in range(G // 2):
            place = place_of(h, 0, True, j)
            for c, col, at in segments(h):
                sends[0][k % 2, h, j, :, at:at + W] = res[k % (LAG + 1), slab_at(c, place), :, col:col + W]
        exchange(k, h, 0).start()

    def emit(k, m):
        rows = pl.ds(pl.multiple_of(m * S + k * rk, rk), rk)
        return pltpu.make_async_copy(og.at[rows], out.at[rows], out_sem.at[k % 2, m])

    def receive(k, i):
        for h in range(2):
            exchange(k, h, i).wait_recv()
            if i == nb - 1:
                for c, col, at in segments(h):
                    if i == 0:
                        v = res[k % (LAG + 1), slab_at(c, g), :, col:col + W].astype(jnp.float32)
                    else:
                        v = curs[i - 1][k % LAG, h, 0, :, at:at + W]
                    v = (v + recvs[i][k, h, 0, :, at:at + W].astype(jnp.float32)).astype(jnp.bfloat16)
                    for m in range(q):
                        og[pl.ds(pl.multiple_of(m * S + k * rk, rk), rk), col:col + W] = v[m * rk:(m + 1) * rk]
                if h == 1:
                    for m in range(q):
                        @pl.when(k >= 2)
                        def _():
                            emit(k - 2, m).wait()

                        emit(k, m).start()
                continue
            reuse(k, h, i + 1)
            count = 1 << (nb - i - 2)
            mine = bit(order(h)[i + 1])
            for keep in (0, 1):
                side = mine if keep else 1 - mine
                for j in range(count):
                    at_j = side * count + j
                    place = place_of(h, i, False, at_j)
                    for c, col, at in segments(h):
                        if i == 0:
                            v = res[k % (LAG + 1), slab_at(c, place), :, col:col + W].astype(jnp.float32)
                        else:
                            v = curs[i - 1][k % LAG, h, at_j, :, at:at + W]
                        v = v + recvs[i][k, h, at_j, :, at:at + W].astype(jnp.float32)
                        if keep:
                            curs[i][k % LAG, h, j, :, at:at + W] = v
                        else:
                            sends[i + 1][k % 2, h, j, :, at:at + W] = v.astype(jnp.bfloat16)
                if not keep:
                    exchange(k, h, i + 1).start()

    def step(t, _):
        ahead = t + 1 < NC

        @pl.when(t < NC)
        def _():
            wait_sibling(t)

            @pl.when(t >= 2)
            def _():
                drain_gather(t - 2)

            @pl.when(ahead & jnp.logical_not(ends))
            def _():
                forward(t + 1, 1, start, True)

            for h in range(2):
                cols = slice(h * Nh, (h + 1) * Nh)
                v = jnp.dot(ga[t].reshape(M, T), cotv[:, cols], preferred_element_type=jnp.float32)
                res[t % (LAG + 1), :, :, cols] = v.astype(jnp.bfloat16).reshape(G, R, Nh)
                first_send(t, h)

            @pl.when(ahead & ends)
            def _():
                forward(t + 1, 1, start, True)

            @pl.when(ahead)
            def _():
                forward(t + 1, 2, start, True)

        for i in range(nb - 1, -1, -1):
            k = t - LAG * (i + 1)

            @pl.when((k >= 0) & (k < NC))
            def _():
                receive(k, i)

        @pl.when(ahead)
        def _():
            for d in range(3, L):
                forward(t + 1, d, start, True)

        @pl.when(t + LEAD < NC)
        def _():
            own(t + LEAD, start)

        return 0

    lax.fori_loop(0, NC + nb * LAG, step, 0)
    for d in range(1, F):
        ss_copy(f, (f + d) % F, d).wait_send()
    for k in range(NC - 2, NC):
        drain_gather(k)
        for m in range(q):
            emit(k, m).wait()
    for i in range(nb):
        for h in range(2):
            for k in (NC - 2, NC - 1):
                exchange(k, h, i).wait_send()


def gradient(G, F, owners, gain, x, cot, NC=32, LAG=3, LEAD=4):
    NC = min(NC, x.shape[1] // 16)
    T, S = x.shape
    N = cot.shape[1]
    nb = G.bit_length() - 1
    L, q, rk, Nh = F // 2, F // G, S // NC, N // 2
    R = q * rk
    slab = S * F // G
    bf, f32 = jnp.bfloat16, jnp.float32
    counts = [G >> (i + 1) for i in range(nb)]
    dma = pltpu.SemaphoreType.DMA
    return pl.pallas_call(
        functools.partial(grad_kernel, G, F, NC, LAG, LEAD),
        out_shape=jax.ShapeDtypeStruct((slab, N), bf),
        in_specs=[
            pl.BlockSpec(memory_space=pltpu.SMEM),
            pl.BlockSpec(memory_space=pltpu.VMEM),
            pl.BlockSpec(memory_space=pl.ANY),
            pl.BlockSpec(memory_space=pl.ANY),
        ],
        out_specs=ANY,
        scratch_shapes=[
            pltpu.VMEM((slab, N), bf),
            pltpu.VMEM((T, S), bf),
            pltpu.VMEM((S, 128), f32),
            pltpu.VMEM((T, 128), f32),
            pltpu.VMEM((T, N), bf),
            pltpu.VMEM((NC, F, rk, T), bf),
            pltpu.VMEM((F, 1, T), f32),
            pltpu.VMEM((LAG + 1, G, R, N), bf),
        ]
        + [pltpu.VMEM((2, 2, n, R, Nh), bf) for n in counts]
        + [pltpu.VMEM((NC, 2, n, R, Nh), bf) for n in counts]
        + [pltpu.VMEM((LAG, 2, n, R, Nh), f32) for n in counts[1:]]
        + [
            dma((2,)),
            dma((2, q)),
            dma((F - 1,)),
            dma((F,)),
            dma((RING, 5)),
            dma((4, L, 3)),
            dma((NC, F)),
            dma((nb, 2, 2)),
            dma((nb, NC, 2)),
        ],
        compiler_params=pltpu.CompilerParams(
            collective_id=0, has_side_effects=True, vmem_limit_bytes=VMEM_LIMIT
        ),
        cost_estimate=pl.CostEstimate(flops=2 * T * S * F * N, bytes_accessed=2 * (T * S + T * N + slab * N), transcendentals=0),
        name="gradient_step",
    )(owners, gain, x, cot)


SCALE_EPSILON = 1e-06
DECAY_RATE = 0.95
RIDGE_TERM = 1e-06
C0 = 1.5625
C1 = -0.3125 - 3125.0 / 4096.0
C2 = 3125.0 / 4096.0
C3 = -1250.0 / 4096.0
C4 = 250.0 / 4096.0
C5 = -25.0 / 4096.0
C6 = 1.0 / 4096.0


def dot(a, b, dims=(((1,), (0,)), ((), ()))):
    return lax.dot_general(a, b, dims, preferred_element_type=jnp.float32)


def inverse_fourth_root(statistic):
    rows = lax.broadcasted_iota(jnp.int32, statistic.shape, 0)
    cols = lax.broadcasted_iota(jnp.int32, statistic.shape, 1)
    diagonal = rows == cols
    matrix = statistic + jnp.where(diagonal, RIDGE_TERM, 0.0)
    scaling = 2.5 * lax.rsqrt(jnp.sum(matrix * matrix, keepdims=True))
    m1 = scaling * matrix
    m1_low = m1.astype(jnp.bfloat16)
    m2 = dot(m1_low, m1_low)
    m3 = dot(m2.astype(jnp.bfloat16), m1_low)
    upper = dot(
        m3.astype(jnp.bfloat16), (C4 * m1 + C5 * m2 + C6 * m3).astype(jnp.bfloat16)
    )
    total = C1 * m1 + C2 * m2 + C3 * m3 + upper + jnp.where(diagonal, C0, 0.0)
    return jnp.sqrt(jnp.sqrt(scaling)) * total


def condition_kernel(G, g_ref, li_ref, ri_ref, *rest):
    outs, held = rest[-G - 1:-1], rest[-1]
    me = lax.axis_index("group")
    grad = g_ref[...]
    half = dot(li_ref[...].astype(jnp.bfloat16), grad)
    conditioned = dot(half.astype(jnp.bfloat16), ri_ref[...].astype(jnp.bfloat16))
    mean = jnp.sum(conditioned * conditioned, keepdims=True) * (1.0 / conditioned.size)
    held[...] = (conditioned * lax.rsqrt(mean + SCALE_EPSILON)).astype(jnp.bfloat16)
    rows = BLK // G
    for m in range(G):
        outs[m][...] = held[pl.ds(pl.multiple_of((me ^ m) * rows, rows), rows), :]


def condition(G, unit, grad, left, right, after):
    r, first, count = unit
    N = count * BLK
    here = pl.BlockSpec((BLK, BLK), lambda c: (r, first + c))
    part = pl.BlockSpec((BLK // G, BLK), lambda c: (0, c))
    return pl.pallas_call(
        functools.partial(condition_kernel, G),
        grid=(N // BLK,),
        in_specs=[here] * 3 + [ANY] * len(after),
        out_specs=[part] * G,
        out_shape=[jax.ShapeDtypeStruct((BLK // G, N), jnp.bfloat16)] * G,
        scratch_shapes=[pltpu.VMEM((BLK, BLK), jnp.bfloat16)],
        compiler_params=pltpu.CompilerParams(
            dimension_semantics=("arbitrary",), vmem_limit_bytes=VMEM_LIMIT
        ),
        cost_estimate=pl.CostEstimate(
            flops=(N // BLK) * 2 * 2 * BLK**3, bytes_accessed=(N // BLK) * 12 * BLK * BLK, transcendentals=0
        ),
        name="condition_step",
    )(grad, left, right, *after)


def stats_kernel(r, refresh, g_ref, ls_ref, rs_ref, li_ref, ri_ref, *rest):
    la_ref, ra_ref, ln_ref, rn_ref, token = rest[-5:]
    token[...] = jnp.zeros_like(token)
    grad = g_ref[...]
    la_ref[...] = DECAY_RATE * ls_ref[...] + (1.0 - DECAY_RATE) * dot(
        grad, grad, (((1,), (1,)), ((), ()))
    )
    ra_ref[...] = DECAY_RATE * rs_ref[...] + (1.0 - DECAY_RATE) * dot(
        grad, grad, (((0,), (0,)), ((), ()))
    )
    flag = refresh[r, pl.program_id(0)]

    @pl.when(flag > 0)
    def _():
        ln_ref[...] = inverse_fourth_root(la_ref[...])
        rn_ref[...] = inverse_fourth_root(ra_ref[...])

    @pl.when(flag <= 0)
    def _():
        ln_ref[...] = li_ref[...]
        rn_ref[...] = ri_ref[...]


def stats(r, grad, refresh, states, previous, after):
    slab_rows, N = states[0].shape
    col_blocks = N // BLK
    here = pl.BlockSpec((BLK, BLK), lambda c, flags: (r, c))
    held = [ANY] * (len(previous) + len(after))
    whole = jax.ShapeDtypeStruct((slab_rows, N), jnp.float32)
    return pl.pallas_call(
        functools.partial(stats_kernel, r),
        grid_spec=pltpu.PrefetchScalarGridSpec(
            num_scalar_prefetch=1,
            grid=(col_blocks,),
            in_specs=[here] * 5 + held,
            out_specs=[here] * 4 + [pl.BlockSpec((8, 128), lambda c, flags: (0, 0))],
        ),
        out_shape=[whole] * 4 + [jax.ShapeDtypeStruct((8, 128), jnp.float32)],
        input_output_aliases={6 + i: i for i in range(len(previous))},
        compiler_params=pltpu.CompilerParams(
            dimension_semantics=("arbitrary",), vmem_limit_bytes=VMEM_LIMIT
        ),
        cost_estimate=pl.CostEstimate(
            flops=col_blocks * 8 * 2 * BLK**3,
            bytes_accessed=col_blocks * 9 * 4 * BLK * BLK,
            transcendentals=0,
        ),
        name="stats_step",
    )(refresh, grad, *states, *previous, *after)


def relay_kernel(G, first, owners, *refs):
    ins, outs = refs[:G], refs[-G:]
    me = lax.axis_index("group")
    c = first + pl.program_id(0)
    for m in range(G):
        wanted = owners[c, me ^ m] ^ me
        for k in range(G):
            @pl.when(wanted == k)
            def _():
                outs[m][...] = ins[k][...]


def relay(G, unit, owners, parts, after):
    rows, N = parts[0].shape
    part = pl.BlockSpec((rows, BLK), lambda c, own: (0, c))
    return pl.pallas_call(
        functools.partial(relay_kernel, G, unit[1]),
        grid_spec=pltpu.PrefetchScalarGridSpec(
            num_scalar_prefetch=1, grid=(N // BLK,), in_specs=[part] * G + [ANY] * len(after), out_specs=[part] * G
        ),
        out_shape=[jax.ShapeDtypeStruct((rows, N), jnp.bfloat16)] * G,
        compiler_params=pltpu.CompilerParams(
            dimension_semantics=("arbitrary",), vmem_limit_bytes=VMEM_LIMIT
        ),
        cost_estimate=pl.CostEstimate(flops=0, bytes_accessed=4 * G * rows * N, transcendentals=0),
        name="relay_step",
    )(owners, *parts, *after)


def place_kernel(G, *refs):
    ins, out = refs[:G], refs[-1]
    me = lax.axis_index("group")
    rows = BLK // G
    for m in range(G):
        out[pl.ds(pl.multiple_of((me ^ m) * rows, rows), rows), :] = ins[m][...]


def place(G, unit, shape, parts, previous, after):
    rows, N = parts[0].shape
    r, first = unit[:2]
    part = pl.BlockSpec((rows, BLK), lambda c: (0, c))
    return pl.pallas_call(
        functools.partial(place_kernel, G),
        grid=(N // BLK,),
        in_specs=[part] * G + [ANY] * (len(previous) + len(after)),
        out_specs=pl.BlockSpec((BLK, BLK), lambda c: (r, first + c)),
        out_shape=jax.ShapeDtypeStruct(shape, jnp.bfloat16),
        input_output_aliases={G: 0} if previous else {},
        compiler_params=pltpu.CompilerParams(
            dimension_semantics=("arbitrary",), vmem_limit_bytes=VMEM_LIMIT
        ),
        cost_estimate=pl.CostEstimate(flops=0, bytes_accessed=4 * BLK * N, transcendentals=0),
        name="place_step",
    )(*parts, *previous, *after)


def swap(G, parts):
    out = [parts[0]]
    for m in range(1, G):
        out.append(lax.ppermute(parts[m], "group", [(i, i ^ m) for i in range(G)]))
    return out


def cut(count, blocks):
    units = []
    for r in range(count):
        cuts = [0, blocks]
        if blocks > 1 and r == 0:
            cuts = [0, blocks // 2, blocks]
        units += [(r, lo, hi - lo) for lo, hi in zip(cuts, cuts[1:])]
    return units


def body(G, F, inputs, norm_gain, cotangent, owners, refresh, *states):
    slab_rows, N = states[0].shape
    own = gradient(G, F, owners, norm_gain, inputs, cotangent)
    count, blocks = slab_rows // BLK, N // BLK
    units = cut(count, blocks)
    sent, back, after = [], [], ()
    for unit in units:
        parts = condition(G, unit, own, states[2], states[3], after)
        after = (parts[0],)
        sent.append(swap(G, parts))
    previous = ()
    for r in range(count):
        *previous, token = stats(r, own, refresh, states, tuple(previous), after)
        after = (token,)
        if r == 0:
            for unit, parts in zip(units, sent):
                parts = relay(G, unit, owners, parts, after)
                after = (parts[0],)
                back.append(swap(G, parts))
    update = ()
    for unit, parts in zip(units, back):
        update = (place(G, unit, (slab_rows, N), parts, update, after),)
    return (*update, *previous)


def solution(mesh):
    spec = P("group", "fsdp")
    in_specs = (spec, P("fsdp"), spec, P("fsdp", None), spec, spec, spec, spec, spec)
    G, F = mesh.shape["group"], mesh.shape["fsdp"]

    def whole(*args):
        def local(*blocks_of):
            return body(G, F, *blocks_of)

        step = jax.shard_map(
            local, mesh=mesh, in_specs=in_specs, out_specs=(spec,) * 5, check_vma=False
        )
        return step(*args)

    return whole
```

```python
import functools
import jax
import jax.numpy as jnp
from jax import lax
from jax.experimental import pallas as pl
from jax.experimental.pallas import tpu as pltpu
from jax.sharding import PartitionSpec as P


BLK = 512
ANY = pl.BlockSpec(memory_space=pl.ANY)
VMEM_LIMIT = 62 * 1024 * 1024
VMEM_ALL = 67043328
NORM_EPSILON = 1e-05
MESH = pl.DeviceIdType.MESH
RING = 8


def remote(src, dst, send_sem, recv_sem, device):
    return pltpu.make_async_remote_copy(
        src_ref=src, dst_ref=dst, send_sem=send_sem, recv_sem=recv_sem,
        device_id=device, device_id_type=MESH,
    )


def grad_kernel(G, F, NC, LAG, LEAD, owners, gain, x_hbm, cot_hbm, out, og, xbuf, gcol, scol, cotv, ga, ssall, res, *rest):
    nb = G.bit_length() - 1
    sends, recvs, curs = rest[:nb], rest[nb:2 * nb], rest[2 * nb:3 * nb - 1]
    lsem, out_sem, ss_send, ss_recv, go, gf, gr, rs_send, rs_recv = rest[3 * nb - 1:]
    T, S = xbuf.shape
    N = cotv.shape[1]
    D = S * F
    L, q, rk, Nh = F // 2, F // G, S // NC, N // 2
    R, M = q * rk, F * rk
    W = min(BLK, Nh)
    g, f = lax.axis_index("group"), lax.axis_index("fsdp")
    l, core = f // 2, f % 2
    sib = f + 1 - 2 * core

    def bit(b):
        return (g // (1 << b)) % 2

    def partner(b):
        return g + (1 - 2 * bit(b)) * (1 << b)

    x_copy = pltpu.make_async_copy(x_hbm, xbuf, lsem.at[0])
    x_copy.start()
    cot_copy = pltpu.make_async_copy(cot_hbm, cotv, lsem.at[1])
    cot_copy.start()

    barrier = pltpu.get_barrier_semaphore()
    for d in range(1, F):
        pl.semaphore_signal(barrier, inc=1, device_id=(g, (f + d) % F), device_id_type=MESH)
    for b in range(nb):
        pl.semaphore_signal(barrier, inc=1, device_id=(partner(b), f), device_id_type=MESH)

    gcol[...] = jnp.broadcast_to(gain[...].astype(jnp.float32)[None, :], (128, S)).T
    x_copy.wait()
    TT = 256
    for i in range(T // TT):
        at = slice(i * TT, (i + 1) * TT)
        v = xbuf[at, :].astype(jnp.float32).T
        ssall[f, :, at] = jnp.sum(v * v, axis=0, keepdims=True)
        v = (v * gcol[:, :1]).astype(jnp.bfloat16)
        for k in range(NC):
            ga[k, f, :, at] = v[k * rk:(k + 1) * rk]
    pl.semaphore_wait(barrier, F - 1 + nb)

    def ss_copy(slot, peer, d):
        return remote(ssall.at[slot], ssall.at[slot], ss_send.at[d - 1], ss_recv.at[slot], (g, peer))

    def piece(k, shard, send_sem, peer):
        return remote(ga.at[k, shard], ga.at[k, shard], send_sem, gr.at[k, shard], (g, peer))

    def pass_on(k, src, sems, sides, then):
        shard = 2 * src + core
        for m, side in enumerate(sides):
            for hop in (1, 2):
                peer = l + side * hop

                @pl.when((peer >= 0) & (peer <= L - 1))
                def _():
                    then(piece(k, shard, sems.at[2 * m + hop - 1], f + 2 * side * hop))

        then(piece(k, shard, sems.at[2 * len(sides)], sib))

    def own(k, then):
        pass_on(k, l, go.at[k % RING], (1, -1), then)

    def forward(k, d, then, receive):
        for side in (1, -1):
            src = l - side * d

            @pl.when((src >= 0) & (src <= L - 1))
            def _():
                if receive:
                    piece(k, 2 * src + core, go.at[0, 0], sib).wait_recv()
                pass_on(k, src, gf.at[k % 4, src], (side,) if d % 2 == 0 else (), then)

    def start(copy):
        copy.start()

    def finish(copy):
        copy.wait_send()

    def wait_sibling(k):
        for src in range(L):
            piece(k, 2 * src + 1 - core, go.at[0, 0], sib).wait_recv()

    def drain_gather(k):
        own(k, finish)
        for d in range(1, L):
            forward(k, d, finish, False)

    for d in range(1, F):
        ss_copy(f, (f + d) % F, d).start()
    own(0, start)
    own(1, start)
    for d in range(1, F):
        peer = (f + d) % F
        ss_copy(peer, peer, d).wait_recv()
    scale = lax.rsqrt(jnp.sum(ssall[...], axis=0) * (1.0 / D) + NORM_EPSILON)
    scol[...] = jnp.broadcast_to(scale, (128, T)).T
    cot_copy.wait()

    def scale_cotangent(i, _):
        rows = pl.ds(pl.multiple_of(i * 256, 256), 256)
        cotv[rows, :] = (cotv[rows, :].astype(jnp.float32) * scol[rows, :1]).astype(jnp.bfloat16)
        return 0

    def forward_all(k):
        for d in range(1, L):
            forward(k, d, start, True)

    lax.fori_loop(0, T // 256, scale_cotangent, 0)
    forward_all(0)
    for k in range(2, min(LEAD, NC)):
        own(k, start)
    ends = (l == 0) | (l == L - 1)

    def slab_at(c, place):
        found = jnp.int32(0)
        for s in range(1, G):
            found = jnp.where(owners[c, s] == place, s, found)
        return found

    def order(h):
        return list(range(nb)) if h == 0 else list(range(nb))[::-1]

    def place_of(h, i, flip, j):
        bits = order(h)
        place = jnp.int32(0)
        for m in range(i + 1):
            mine = bit(bits[m])
            place = place + (1 - mine if (flip and m == i) else mine) * (1 << bits[m])
        left = bits[i + 1:]
        for m, b in enumerate(left):
            place = place + ((j // (1 << (len(left) - 1 - m))) % 2) * (1 << b)
        return place

    def exchange(k, h, i):
        return remote(sends[i].at[k % 2, h], recvs[i].at[k, h], rs_send.at[i, k % 2, h], rs_recv.at[i, k, h],
                      (partner(order(h)[i]), f))

    def reuse(k, h, i):
        @pl.when(k >= 2)
        def _():
            exchange(k - 2, h, i).wait_send()

    def segments(h):
        for n in range(Nh // W):
            yield (h * Nh + n * W) // BLK, h * Nh + n * W, n * W

    def first_send(k, h):
        reuse(k, h, 0)
        for j in range(G // 2):
            place = place_of(h, 0, True, j)
            for c, col, at in segments(h):
                sends[0][k % 2, h, j, :, at:at + W] = res[k % (LAG + 1), slab_at(c, place), :, col:col + W]
        exchange(k, h, 0).start()

    def emit(k, m):
        rows = pl.ds(pl.multiple_of(m * S + k * rk, rk), rk)
        return pltpu.make_async_copy(og.at[rows], out.at[rows], out_sem.at[k % 2, m])

    def receive(k, i):
        for h in range(2):
            exchange(k, h, i).wait_recv()
            if i == nb - 1:
                for c, col, at in segments(h):
                    if i == 0:
                        v = res[k % (LAG + 1), slab_at(c, g), :, col:col + W].astype(jnp.float32)
                    else:
                        v = curs[i - 1][k % LAG, h, 0, :, at:at + W]
                    v = (v + recvs[i][k, h, 0, :, at:at + W].astype(jnp.float32)).astype(jnp.bfloat16)
                    for m in range(q):
                        og[pl.ds(pl.multiple_of(m * S + k * rk, rk), rk), col:col + W] = v[m * rk:(m + 1) * rk]
                if h == 1:
                    for m in range(q):
                        @pl.when(k >= 2)
                        def _():
                            emit(k - 2, m).wait()

                        emit(k, m).start()
                continue
            reuse(k, h, i + 1)
            count = 1 << (nb - i - 2)
            mine = bit(order(h)[i + 1])
            for keep in (0, 1):
                side = mine if keep else 1 - mine
                for j in range(count):
                    at_j = side * count + j
                    place = place_of(h, i, False, at_j)
                    for c, col, at in segments(h):
                        if i == 0:
                            v = res[k % (LAG + 1), slab_at(c, place), :, col:col + W].astype(jnp.float32)
                        else:
                            v = curs[i - 1][k % LAG, h, at_j, :, at:at + W]
                        v = v + recvs[i][k, h, at_j, :, at:at + W].astype(jnp.float32)
                        if keep:
                            curs[i][k % LAG, h, j, :, at:at + W] = v
                        else:
                            sends[i + 1][k % 2, h, j, :, at:at + W] = v.astype(jnp.bfloat16)
                if not keep:
                    exchange(k, h, i + 1).start()

    def step(t, _):
        ahead = t + 1 < NC

        @pl.when(t < NC)
        def _():
            wait_sibling(t)

            @pl.when(t >= 2)
            def _():
                drain_gather(t - 2)

            @pl.when(ahead & jnp.logical_not(ends))
            def _():
                forward(t + 1, 1, start, True)

            for h in range(2):
                cols = slice(h * Nh, (h + 1) * Nh)
                v = jnp.dot(ga[t].reshape(M, T), cotv[:, cols], preferred_element_type=jnp.float32)
                res[t % (LAG + 1), :, :, cols] = v.astype(jnp.bfloat16).reshape(G, R, Nh)
                first_send(t, h)

            @pl.when(ahead & ends)
            def _():
                forward(t + 1, 1, start, True)

            @pl.when(ahead)
            def _():
                forward(t + 1, 2, start, True)

        for i in range(nb - 1, -1, -1):
            k = t - LAG * (i + 1)

            @pl.when((k >= 0) & (k < NC))
            def _():
                receive(k, i)

        @pl.when(ahead)
        def _():
            for d in range(3, L):
                forward(t + 1, d, start, True)

        @pl.when(t + LEAD < NC)
        def _():
            own(t + LEAD, start)

        return 0

    lax.fori_loop(0, NC + nb * LAG, step, 0)
    for d in range(1, F):
        ss_copy(f, (f + d) % F, d).wait_send()
    for k in range(NC - 2, NC):
        drain_gather(k)
        for m in range(q):
            emit(k, m).wait()
    for i in range(nb):
        for h in range(2):
            for k in (NC - 2, NC - 1):
                exchange(k, h, i).wait_send()


def gradient(G, F, owners, gain, x, cot, NC=32, LAG=3, LEAD=4):
    NC = min(NC, x.shape[1] // 16)
    T, S = x.shape
    N = cot.shape[1]
    nb = G.bit_length() - 1
    L, q, rk, Nh = F // 2, F // G, S // NC, N // 2
    R = q * rk
    slab = S * F // G
    bf, f32 = jnp.bfloat16, jnp.float32
    counts = [G >> (i + 1) for i in range(nb)]
    dma = pltpu.SemaphoreType.DMA
    return pl.pallas_call(
        functools.partial(grad_kernel, G, F, NC, LAG, LEAD),
        out_shape=jax.ShapeDtypeStruct((slab, N), bf),
        in_specs=[
            pl.BlockSpec(memory_space=pltpu.SMEM),
            pl.BlockSpec(memory_space=pltpu.VMEM),
            pl.BlockSpec(memory_space=pl.ANY),
            pl.BlockSpec(memory_space=pl.ANY),
        ],
        out_specs=ANY,
        scratch_shapes=[
            pltpu.VMEM((slab, N), bf),
            pltpu.VMEM((T, S), bf),
            pltpu.VMEM((S, 128), f32),
            pltpu.VMEM((T, 128), f32),
            pltpu.VMEM((T, N), bf),
            pltpu.VMEM((NC, F, rk, T), bf),
            pltpu.VMEM((F, 1, T), f32),
            pltpu.VMEM((LAG + 1, G, R, N), bf),
        ]
        + [pltpu.VMEM((2, 2, n, R, Nh), bf) for n in counts]
        + [pltpu.VMEM((NC, 2, n, R, Nh), bf) for n in counts]
        + [pltpu.VMEM((LAG, 2, n, R, Nh), f32) for n in counts[1:]]
        + [
            dma((2,)),
            dma((2, q)),
            dma((F - 1,)),
            dma((F,)),
            dma((RING, 5)),
            dma((4, L, 3)),
            dma((NC, F)),
            dma((nb, 2, 2)),
            dma((nb, NC, 2)),
        ],
        compiler_params=pltpu.CompilerParams(
            collective_id=0, has_side_effects=True, vmem_limit_bytes=VMEM_LIMIT
        ),
        cost_estimate=pl.CostEstimate(flops=2 * T * S * F * N, bytes_accessed=2 * (T * S + T * N + slab * N), transcendentals=0),
        name="gradient_step",
    )(owners, gain, x, cot)


SCALE_EPSILON = 1e-06
DECAY_RATE = 0.95
RIDGE_TERM = 1e-06
C0 = 1.5625
C1 = -0.3125 - 3125.0 / 4096.0
C2 = 3125.0 / 4096.0
C3 = -1250.0 / 4096.0
C4 = 250.0 / 4096.0
C5 = -25.0 / 4096.0
C6 = 1.0 / 4096.0


def dot(a, b, dims=(((1,), (0,)), ((), ()))):
    return lax.dot_general(a, b, dims, preferred_element_type=jnp.float32)


def inverse_fourth_root(statistic):
    rows = lax.broadcasted_iota(jnp.int32, statistic.shape, 0)
    cols = lax.broadcasted_iota(jnp.int32, statistic.shape, 1)
    diagonal = rows == cols
    matrix = statistic + jnp.where(diagonal, RIDGE_TERM, 0.0)
    scaling = 2.5 * lax.rsqrt(jnp.sum(matrix * matrix, keepdims=True))
    m1 = scaling * matrix
    m1_low = m1.astype(jnp.bfloat16)
    m2 = dot(m1_low, m1_low)
    m3 = dot(m2.astype(jnp.bfloat16), m1_low)
    upper = dot(
        m3.astype(jnp.bfloat16), (C4 * m1 + C5 * m2 + C6 * m3).astype(jnp.bfloat16)
    )
    total = C1 * m1 + C2 * m2 + C3 * m3 + upper + jnp.where(diagonal, C0, 0.0)
    return jnp.sqrt(jnp.sqrt(scaling)) * total


def condition_kernel(G, g_ref, li_ref, ri_ref, *rest):
    outs, held = rest[-G - 1:-1], rest[-1]
    me = lax.axis_index("group")
    grad = g_ref[...]
    half = dot(li_ref[...].astype(jnp.bfloat16), grad)
    conditioned = dot(half.astype(jnp.bfloat16), ri_ref[...].astype(jnp.bfloat16))
    mean = jnp.sum(conditioned * conditioned, keepdims=True) * (1.0 / conditioned.size)
    held[...] = (conditioned * lax.rsqrt(mean + SCALE_EPSILON)).astype(jnp.bfloat16)
    rows = BLK // G
    for m in range(G):
        outs[m][...] = held[pl.ds(pl.multiple_of((me ^ m) * rows, rows), rows), :]


def condition(G, unit, grad, left, right, after):
    r, first, count = unit
    N = count * BLK
    here = pl.BlockSpec((BLK, BLK), lambda c: (r, first + c))
    part = pl.BlockSpec((BLK // G, BLK), lambda c: (0, c))
    return pl.pallas_call(
        functools.partial(condition_kernel, G),
        grid=(N // BLK,),
        in_specs=[here] * 3 + [ANY] * len(after),
        out_specs=[part] * G,
        out_shape=[jax.ShapeDtypeStruct((BLK // G, N), jnp.bfloat16)] * G,
        scratch_shapes=[pltpu.VMEM((BLK, BLK), jnp.bfloat16)],
        compiler_params=pltpu.CompilerParams(
            dimension_semantics=("arbitrary",), vmem_limit_bytes=VMEM_ALL
        ),
        cost_estimate=pl.CostEstimate(
            flops=(N // BLK) * 2 * 2 * BLK**3, bytes_accessed=(N // BLK) * 12 * BLK * BLK, transcendentals=0
        ),
        name="condition_step",
    )(grad, left, right, *after)


def stats_kernel(r, refresh, g_ref, ls_ref, rs_ref, li_ref, ri_ref, *rest):
    la_ref, ra_ref, ln_ref, rn_ref, token = rest[-5:]
    token[...] = jnp.zeros_like(token)
    grad = g_ref[...]
    la_ref[...] = DECAY_RATE * ls_ref[...] + (1.0 - DECAY_RATE) * dot(
        grad, grad, (((1,), (1,)), ((), ()))
    )
    ra_ref[...] = DECAY_RATE * rs_ref[...] + (1.0 - DECAY_RATE) * dot(
        grad, grad, (((0,), (0,)), ((), ()))
    )
    flag = refresh[r, pl.program_id(0)]

    @pl.when(flag > 0)
    def _():
        ln_ref[...] = inverse_fourth_root(la_ref[...])
        rn_ref[...] = inverse_fourth_root(ra_ref[...])

    @pl.when(flag <= 0)
    def _():
        ln_ref[...] = li_ref[...]
        rn_ref[...] = ri_ref[...]


def stats(r, grad, refresh, states, previous, after):
    slab_rows, N = states[0].shape
    col_blocks = N // BLK
    here = pl.BlockSpec((BLK, BLK), lambda c, flags: (r, c))
    held = [ANY] * (len(previous) + len(after))
    whole = jax.ShapeDtypeStruct((slab_rows, N), jnp.float32)
    return pl.pallas_call(
        functools.partial(stats_kernel, r),
        grid_spec=pltpu.PrefetchScalarGridSpec(
            num_scalar_prefetch=1,
            grid=(col_blocks,),
            in_specs=[here] * 5 + held,
            out_specs=[here] * 4 + [pl.BlockSpec((8, 128), lambda c, flags: (0, 0))],
        ),
        out_shape=[whole] * 4 + [jax.ShapeDtypeStruct((8, 128), jnp.float32)],
        input_output_aliases={6 + i: i for i in range(len(previous))},
        compiler_params=pltpu.CompilerParams(
            dimension_semantics=("arbitrary",), vmem_limit_bytes=VMEM_ALL
        ),
        cost_estimate=pl.CostEstimate(
            flops=col_blocks * 8 * 2 * BLK**3,
            bytes_accessed=col_blocks * 9 * 4 * BLK * BLK,
            transcendentals=0,
        ),
        name="stats_step",
    )(refresh, grad, *states, *previous, *after)


def relay_kernel(G, first, owners, *refs):
    ins, outs = refs[:G], refs[-G:]
    me = lax.axis_index("group")
    c = first + pl.program_id(0)
    for m in range(G):
        wanted = owners[c, me ^ m] ^ me
        for k in range(G):
            @pl.when(wanted == k)
            def _():
                outs[m][...] = ins[k][...]


def relay(G, unit, owners, parts, after):
    rows, N = parts[0].shape
    part = pl.BlockSpec((rows, BLK), lambda c, own: (0, c))
    return pl.pallas_call(
        functools.partial(relay_kernel, G, unit[1]),
        grid_spec=pltpu.PrefetchScalarGridSpec(
            num_scalar_prefetch=1, grid=(N // BLK,), in_specs=[part] * G + [ANY] * len(after), out_specs=[part] * G
        ),
        out_shape=[jax.ShapeDtypeStruct((rows, N), jnp.bfloat16)] * G,
        compiler_params=pltpu.CompilerParams(
            dimension_semantics=("arbitrary",), vmem_limit_bytes=VMEM_ALL
        ),
        cost_estimate=pl.CostEstimate(flops=0, bytes_accessed=4 * G * rows * N, transcendentals=0),
        name="relay_step",
    )(owners, *parts, *after)


def place_kernel(G, *refs):
    ins, out = refs[:G], refs[-1]
    me = lax.axis_index("group")
    rows = BLK // G
    for m in range(G):
        out[pl.ds(pl.multiple_of((me ^ m) * rows, rows), rows), :] = ins[m][...]


def place(G, unit, shape, parts, previous, after):
    rows, N = parts[0].shape
    r, first = unit[:2]
    wide = BLK * (2 if N % (2 * BLK) == 0 and first % 2 == 0 else 1)
    start = first * BLK // wide
    part = pl.BlockSpec((rows, wide), lambda c: (0, c))
    return pl.pallas_call(
        functools.partial(place_kernel, G),
        grid=(N // wide,),
        in_specs=[part] * G + [ANY] * (len(previous) + len(after)),
        out_specs=pl.BlockSpec((BLK, wide), lambda c: (r, start + c)),
        out_shape=jax.ShapeDtypeStruct(shape, jnp.bfloat16),
        input_output_aliases={G: 0} if previous else {},
        compiler_params=pltpu.CompilerParams(
            dimension_semantics=("arbitrary",), vmem_limit_bytes=VMEM_ALL
        ),
        cost_estimate=pl.CostEstimate(flops=0, bytes_accessed=4 * BLK * N, transcendentals=0),
        name="place_step",
    )(*parts, *previous, *after)


def swap(G, parts):
    out = [parts[0]]
    for m in range(1, G):
        out.append(lax.ppermute(parts[m], "group", [(i, i ^ m) for i in range(G)]))
    return out


def cut(count, blocks):
    units = []
    for r in range(count):
        cuts = [0, blocks]
        if blocks > 1 and r == 0:
            cuts = [0, blocks // 2, blocks]
        units += [(r, lo, hi - lo) for lo, hi in zip(cuts, cuts[1:])]
    return units


def body(G, F, inputs, norm_gain, cotangent, owners, refresh, *states):
    slab_rows, N = states[0].shape
    own = gradient(G, F, owners, norm_gain, inputs, cotangent)
    count, blocks = slab_rows // BLK, N // BLK
    units = cut(count, blocks)
    sent, back, after = [], [], ()
    for unit in units:
        parts = condition(G, unit, own, states[2], states[3], after)
        after = (parts[0],)
        sent.append(swap(G, parts))
    previous = ()
    for r in range(count):
        *previous, token = stats(r, own, refresh, states, tuple(previous), after)
        after = (token,)
        if r == 0:
            for unit, parts in zip(units, sent):
                parts = relay(G, unit, owners, parts, after)
                after = (parts[0],)
                back.append(swap(G, parts))
    update = ()
    for unit, parts in zip(units, back):
        update = (place(G, unit, (slab_rows, N), parts, update, after),)
    return (*update, *previous)


def solution(mesh):
    spec = P("group", "fsdp")
    in_specs = (spec, P("fsdp"), spec, P("fsdp", None), spec, spec, spec, spec, spec)
    G, F = mesh.shape["group"], mesh.shape["fsdp"]

    def whole(*args):
        def local(*blocks_of):
            return body(G, F, *blocks_of)

        step = jax.shard_map(
            local, mesh=mesh, in_specs=in_specs, out_specs=(spec,) * 5, check_vma=False
        )
        return step(*args)

    return whole
```
